256 devices in a mesh: pp: 4 (over y_lo, core), ep: 64 (over x, y_hi, z).
Axes of the slice: x: 4, y: 4 (y_hi: 2, y_lo: 2; y = y_hi * 2 + y_lo), z: 8, core: 2. Of those that a mesh axis runs over, the one named last changes fastest.
Arguments:
- fwd_in: bfloat16 [4, 4096, 7168], P('pp', 'ep'), may hold values from -6 to 6
- fwd_ids: int32 [4, 4096, 1], P('pp', 'ep'), may hold values from 0 to 7
- fwd_gates: float32 [4, 4096, 1], P('pp', 'ep'), may hold values from 0.2 to 1.5
- bwd_x: bfloat16 [4, 4096, 7168], P('pp', 'ep'), may hold values from -6 to 6
- bwd_grad: bfloat16 [4, 4096, 7168], P('pp', 'ep'), may hold values from -6 to 6
- bwd_ids: int32 [4, 4096, 1], P('pp', 'ep'), may hold values from 0 to 7
- bwd_gates: float32 [4, 4096, 1], P('pp', 'ep'), may hold values from 0.2 to 1.5
- norm_gain: float32 [4, 7168], P('pp'), may hold values from 0.25 to 1.75
- w_gate: bfloat16 [4, 64, 7168, 128], P('pp', 'ep'), may hold values from -0.0625 to 0.0625
- w_up: bfloat16 [4, 64, 7168, 128], P('pp', 'ep'), may hold values from -0.0625 to 0.0625
- w_down: bfloat16 [4, 64, 128, 7168], P('pp', 'ep'), may hold values from -0.1875 to 0.1875
Outputs:
- fwd_out: bfloat16 [4, 4096, 7168], P('pp', 'ep')
- bwd_out: bfloat16 [4, 4096, 7168], P('pp', 'ep')
The draws below stay inside these ranges and needn't reach their ends.
Inputs may be any that keep to these rules, and one draw needn't show every extreme that they name: `fwd_ids`: each row names one expert. `bwd_ids`: as for fwd_ids.
All inputs are finite; a program needn't handle non-finite values.
Results may differ from the reference program's by a relative error of at most 0.0053.
Values may be sent and summed in bfloat16 or wider, within the bound.
No kernel may reach another device: no remote copies, remote signals or barrier semaphores. Data moves between devices by JAX's collectives and lax.ppermute only.
A program may use at most 128 MiB of HBM per device.

```python
import jax
import jax.numpy as jnp
from jax import lax

D = 7168
HIDDEN_SIZE = 1024
EXPERTS = 8
SLICES = 8
H_DEV = 128
TOP = 1
TOK_DEV = 64
CAP = 3
TOKENS = 4096
N_PP = 4
N_EP = 64


def shard_levels(own_key, dims, cuts, least, top_value):
    gain, own = 1.0, jax.random.fold_in(own_key, 6)
    for dim, shards_of in cuts:
        steps = jnp.exp(jax.random.uniform(jax.random.fold_in(own, dim), (shards_of,), jnp.float32, least / len(cuts), top_value / len(cuts)))
        gain = gain * jnp.repeat(steps, dims[dim] // shards_of).reshape([-1 if axis == dim else 1 for axis in range(len(dims))])
    return gain


def picks_of(key, rows, count, top, lift):
    sequence = jax.random.permutation(jax.random.fold_in(key, 1), count)
    boost = sequence
    for power in range(3):
        boost = boost * boost // count
    boost = boost * lift // count
    tickets = jax.random.randint(jax.random.fold_in(key, 2), (rows, count), 0, 4096) + boost
    fixed_rows = jax.random.permutation(jax.random.fold_in(key, 3), rows)[jnp.arange(count) % rows]
    tickets = jnp.where(jnp.arange(rows)[:, None] == fixed_rows[None, :], 1 << 14, tickets)
    merit = tickets * count + jnp.arange(count)
    return lax.top_k(merit.astype(jnp.int32), top)[1].astype(jnp.int32)


def noise(own_key, dims, scale, bound, pieces=(), kind=jnp.bfloat16):
    level = shard_levels(own_key, dims, pieces, -0.22, 0.18) if pieces else 1.0
    array = jax.random.normal(own_key, dims, jnp.float32) * scale * level
    return jnp.minimum(jnp.maximum(array, -bound), bound).astype(kind)


def setup_inputs(seed: int = 0) -> dict:
    key_of = jax.random.split(jax.random.key(seed), 12)
    return {
        "fwd_in": noise(key_of[0], (N_PP, TOKENS, D), 1.0, 6.0, ((0, 4), (1, 64))),
        "fwd_ids": picks_of(key_of[1], N_PP * TOKENS, EXPERTS, TOP, 2048).reshape((N_PP, TOKENS, TOP)),
        "fwd_gates": jnp.clip(0.2 + 1.3 * jax.random.uniform(key_of[2], (N_PP, TOKENS, TOP), jnp.float32) ** shard_levels(key_of[2], (N_PP, TOKENS, TOP), ((0, 4), (1, 64)), -0.2, 0.2), 0.2, 1.5),
        "bwd_x": noise(key_of[3], (N_PP, TOKENS, D), 1.0, 6.0, ((0, 4), (1, 64))),
        "bwd_grad": noise(key_of[4], (N_PP, TOKENS, D), 1.0, 6.0, ((0, 4), (1, 64))),
        "bwd_ids": picks_of(key_of[5], N_PP * TOKENS, EXPERTS, TOP, 2048).reshape((N_PP, TOKENS, TOP)),
        "bwd_gates": jnp.clip(0.2 + 1.3 * jax.random.uniform(key_of[6], (N_PP, TOKENS, TOP), jnp.float32) ** shard_levels(key_of[6], (N_PP, TOKENS, TOP), ((0, 4), (1, 64)), -0.2, 0.2), 0.2, 1.5),
        "norm_gain": jnp.clip(1.0 + 0.15 * jax.random.normal(key_of[7], (N_PP, D), jnp.float32), 0.25, 1.75),
        "w_gate": noise(key_of[8], (N_PP, N_EP, D, H_DEV), D ** -0.5, 0.0625, ((0, 4), (1, 64))),
        "w_up": noise(key_of[9], (N_PP, N_EP, D, H_DEV), D ** -0.5, 0.0625, ((0, 4), (1, 64))),
        "w_down": noise(key_of[10], (N_PP, N_EP, H_DEV, D), HIDDEN_SIZE ** -0.5, 0.1875, ((0, 4), (1, 64))),
    }


EPSILON = 1e-06

def normalize(row_block):
    values = row_block.astype(jnp.float32)
    scale = lax.rsqrt(lax.optimization_barrier(jnp.mean(values * values, axis=-1, keepdims=True)) + EPSILON)
    return (values, scale)

def slot_owners(expert_ids):
    flat_ids = expert_ids.reshape(N_EP, TOK_DEV * TOP).astype(jnp.int32)
    expert_range = jnp.arange(EXPERTS, dtype=jnp.int32)
    onehot = (flat_ids[:, :, None] == expert_range[None, None, :]).astype(jnp.int32)
    before = jnp.cumsum(onehot, axis=1) - onehot
    slot_index = lax.optimization_barrier(jnp.sum(before * onehot, axis=2)).astype(jnp.int32)
    target = jnp.where(slot_index < CAP, flat_ids * CAP + slot_index, EXPERTS * CAP).astype(jnp.int32)
    source = jnp.broadcast_to(jnp.arange(N_EP, dtype=jnp.int32)[:, None], target.shape)
    assigned = jnp.broadcast_to(jnp.arange(TOK_DEV * TOP, dtype=jnp.int32)[None, :], target.shape)
    slot_table = jnp.full((N_EP, EXPERTS * CAP), -1, dtype=jnp.int32).at[source, target].set(assigned, mode='drop')
    slot_table = slot_table.reshape(N_EP, EXPERTS, CAP).transpose(1, 0, 2).reshape(EXPERTS, N_EP * CAP)
    occupied = slot_table >= 0
    safe_slot = jnp.where(occupied, slot_table, 0).astype(jnp.int32)
    source_device = (jnp.arange(N_EP * CAP, dtype=jnp.int32) // CAP)[None, :]
    token_index = (source_device * TOK_DEV + safe_slot // TOP).astype(jnp.int32)
    top_pick = (safe_slot % TOP).astype(jnp.int32)
    return (token_index, top_pick, occupied)

def forward_expert(operands):
    row_block, gate_mats, up_mats, down_mats = operands
    summed = jnp.zeros((row_block.shape[0], D), jnp.float32)
    for piece in range(SLICES):
        act_gate = jnp.dot(row_block, gate_mats[piece], preferred_element_type=jnp.float32)
        act_up = jnp.dot(row_block, up_mats[piece], preferred_element_type=jnp.float32)
        hidden = (jax.nn.silu(act_gate) * act_up).astype(jnp.bfloat16)
        partial_value = jnp.dot(hidden, down_mats[piece], preferred_element_type=jnp.float32).astype(jnp.bfloat16)
        summed = summed + partial_value.astype(jnp.float32)
    return summed

def backward_expert(operands):
    row_block, grad_block, gate_mats, up_mats, down_mats = operands
    summed = jnp.zeros((row_block.shape[0], D), jnp.float32)
    for piece in range(SLICES):
        act_gate = jnp.dot(row_block, gate_mats[piece], preferred_element_type=jnp.float32)
        act_up = jnp.dot(row_block, up_mats[piece], preferred_element_type=jnp.float32)
        back_hidden = jnp.dot(grad_block, down_mats[piece].T, preferred_element_type=jnp.float32)
        sigmoid_val = jax.nn.sigmoid(act_gate)
        grad_gate = (back_hidden * act_up * sigmoid_val * (1.0 + act_gate * (1.0 - sigmoid_val))).astype(jnp.bfloat16)
        grad_up = (back_hidden * act_gate * sigmoid_val).astype(jnp.bfloat16)
        partial_value = jnp.dot(grad_gate, gate_mats[piece].T, preferred_element_type=jnp.float32)
        partial_value = partial_value + jnp.dot(grad_up, up_mats[piece].T, preferred_element_type=jnp.float32)
        summed = summed + partial_value.astype(jnp.bfloat16).astype(jnp.float32)
    return summed

def reference(fwd_in, fwd_ids, fwd_gates, bwd_x, bwd_grad, bwd_ids, bwd_gates, norm_gain, w_gate, w_up, w_down):
    forward_list = []
    backward_list = []
    for section_index in range(N_PP):
        gate_mats = w_gate[section_index].reshape(EXPERTS, SLICES, D, H_DEV)
        up_mats = w_up[section_index].reshape(EXPERTS, SLICES, D, H_DEV)
        down_mats = w_down[section_index].reshape(EXPERTS, SLICES, H_DEV, D)
        norm_row = norm_gain[section_index]
        arrived = fwd_in[(section_index - 1) % N_PP]
        fwd_values, fwd_scale = normalize(arrived)
        normed_a = (fwd_values * fwd_scale * norm_row).astype(jnp.bfloat16)
        token_index, top_pick, occupied = slot_owners(fwd_ids[section_index])
        picked = jnp.where(occupied[:, :, None], normed_a[token_index], jnp.zeros((), jnp.bfloat16))
        gate_pick = jnp.where(occupied, fwd_gates[section_index][token_index, top_pick], jnp.zeros((), jnp.float32))
        expert_out = lax.map(forward_expert, (picked, gate_mats, up_mats, down_mats))
        contribution = (gate_pick[:, :, None] * expert_out).reshape(-1, D)
        expert_mix = jnp.zeros((TOKENS, D), jnp.float32).at[token_index.reshape(-1)].add(contribution)
        forward_list.append((fwd_values + expert_mix).astype(jnp.bfloat16))
        upstream = bwd_grad[(section_index + 1) % N_PP]
        grad_values = upstream.astype(jnp.float32)
        bwd_values, bwd_scale = normalize(bwd_x[section_index])
        normed_b = (bwd_values * bwd_scale * norm_row).astype(jnp.bfloat16)
        token_index, top_pick, occupied = slot_owners(bwd_ids[section_index])
        picked = jnp.where(occupied[:, :, None], normed_b[token_index], jnp.zeros((), jnp.bfloat16))
        gate_pick = jnp.where(occupied, bwd_gates[section_index][token_index, top_pick], jnp.zeros((), jnp.float32))
        scaled_rows = (gate_pick[:, :, None] * grad_values[token_index]).astype(jnp.bfloat16)
        expert_back = lax.map(backward_expert, (picked, scaled_rows, gate_mats, up_mats, down_mats))
        occupied_f = occupied.astype(jnp.float32)[:, :, None]
        grad_norm = jnp.zeros((TOKENS, D), jnp.float32).at[token_index.reshape(-1)].add((expert_back * occupied_f).reshape(-1, D))
        scaled_grad = norm_row * grad_norm
        norm_back = bwd_scale * scaled_grad - bwd_values * bwd_scale ** 3 * lax.optimization_barrier(jnp.mean(bwd_values * scaled_grad, axis=-1, keepdims=True))
        backward_list.append((grad_values + norm_back).astype(jnp.bfloat16))
    return (jnp.stack(forward_list), jnp.stack(backward_list))
```

```python
import jax
import jax.numpy as jnp
from jax import lax
from jax.sharding import Mesh, PartitionSpec as P

EPSILON = 1e-06
BF16 = jnp.bfloat16
F32 = jnp.float32


def shifted(block, axis, distance):
    count = lax.axis_size(axis)
    route = [(i, (i + distance) % count) for i in range(count)]
    return lax.ppermute(block, axis, route)


def normalize(row_block):
    values = row_block.astype(F32)
    scale = lax.rsqrt(jnp.mean(values * values, axis=-1, keepdims=True) + EPSILON)
    return (values, scale)


def routing(expert_ids, experts, capacity):
    tok_count = expert_ids.shape[1]
    onehot = (lax.broadcasted_iota(jnp.int32, (experts, tok_count), 0) == expert_ids).astype(F32)
    earlier = lax.broadcasted_iota(jnp.int32, (tok_count, tok_count), 0) < lax.broadcasted_iota(
        jnp.int32, (tok_count, tok_count), 1
    )
    before = jnp.dot(onehot, earlier.astype(F32), preferred_element_type=F32)
    slot_index = jnp.sum(before * onehot, axis=0, keepdims=True).astype(jnp.int32)
    target = jnp.where(slot_index < capacity, expert_ids * capacity + slot_index, -1)
    slot_iota = lax.broadcasted_iota(jnp.int32, (experts * capacity, tok_count), 0)
    return slot_iota == target


def pick(selector, rows):
    return jnp.dot(selector.astype(BF16), rows, preferred_element_type=F32)


def unpick(selector, rows):
    return lax.dot_general(
        selector.astype(BF16), rows, (((0,), (0,)), ((), ())), preferred_element_type=F32
    )


def exchange(slot_rows, experts):
    shaped = slot_rows.reshape(experts, -1, slot_rows.shape[-1])
    return lax.all_to_all(shaped, "e", split_axis=0, concat_axis=0, tiled=True).reshape(
        slot_rows.shape
    )


def ring_gather(block):
    count = lax.axis_size("k")
    half = block.shape[1] // 2
    up, down = block, block
    blocks = {0: block}
    for step in range(1, count // 2):
        up = shifted(up, "k", 1)
        down = shifted(down, "k", -1)
        blocks[-step] = up
        blocks[step] = down
    far = jnp.concatenate(
        [shifted(up[:, :half], "k", 1), shifted(down[:, half:], "k", -1)], axis=1
    )
    blocks[count // 2] = far
    return blocks


def ring_reduce(parts):
    count = lax.axis_size("k")
    far = count // 2
    half = parts[far].shape[1] // 2
    down = shifted(parts[far][:, :half], "k", -1)
    up = shifted(parts[far][:, half:], "k", 1)

    def add(a, b):
        return (a.astype(F32) + b.astype(F32)).astype(BF16)

    own_down, own_up = parts[1 - far], parts[far - 1]
    down = jnp.concatenate([add(down, own_down[:, :half]), own_down[:, half:]], axis=1)
    up = jnp.concatenate([own_up[:, :half], add(up, own_up[:, half:])], axis=1)
    for step in range(far - 2, -1, -1):
        down = shifted(down, "k", -1)
        up = shifted(up, "k", 1)
        if step:
            down = add(down, parts[-step])
            up = add(up, parts[step])
    total = parts[0].astype(F32) + down.astype(F32) + up.astype(F32)
    return total.astype(BF16)


def split_rows(rows, keys):
    size = rows.shape[0] // len(keys)
    return {key: rows[i * size : (i + 1) * size] for i, key in enumerate(keys)}


def forward_parts(blocks, keys, gate_mat, up_mat, down_mat):
    rows = jnp.concatenate([blocks[key] for key in keys], axis=0)
    act_gate = jnp.dot(rows, gate_mat, preferred_element_type=F32)
    act_up = jnp.dot(rows, up_mat, preferred_element_type=F32)
    hidden = (jax.nn.silu(act_gate) * act_up).astype(BF16)
    part = jnp.dot(hidden, down_mat, preferred_element_type=F32).astype(BF16)
    return split_rows(part, keys)


def backward_parts(blocks, grads, keys, gate_mat, up_mat, down_mat):
    rows = jnp.concatenate([blocks[key] for key in keys], axis=0)
    grad_rows = jnp.concatenate([grads[key] for key in keys], axis=0)
    act_gate = jnp.dot(rows, gate_mat, preferred_element_type=F32)
    act_up = jnp.dot(rows, up_mat, preferred_element_type=F32)
    back_hidden = lax.dot_general(
        grad_rows, down_mat, (((1,), (1,)), ((), ())), preferred_element_type=F32
    )
    sigma = jax.nn.sigmoid(act_gate)
    grad_gate = (back_hidden * act_up * sigma * (1.0 + act_gate * (1.0 - sigma))).astype(BF16)
    grad_up = (back_hidden * act_gate * sigma).astype(BF16)
    part = lax.dot_general(
        grad_gate, gate_mat, (((1,), (1,)), ((), ())), preferred_element_type=F32
    ) + lax.dot_general(grad_up, up_mat, (((1,), (1,)), ((), ())), preferred_element_type=F32)
    return split_rows(part.astype(BF16), keys)


def body(
    fwd_in, fwd_ids, fwd_gates, bwd_x, bwd_grad, bwd_ids, bwd_gates, norm_gain, w_gate, w_up, w_down
):
    experts = lax.axis_size("e")
    tok_count = fwd_in.shape[1]
    capacity = max(2, tok_count * fwd_ids.shape[2] // 20)
    norm_row = norm_gain
    gate_mat, up_mat, down_mat = w_gate[0, 0], w_up[0, 0], w_down[0, 0]
    arrived = shifted(fwd_in[0], "pp", 1)
    upstream = shifted(bwd_grad[0], "pp", -1)

    bwd_select = routing(bwd_ids.reshape(1, tok_count), experts, capacity)
    bwd_values, bwd_scale = normalize(bwd_x[0])
    normed_b = (bwd_values * bwd_scale * norm_row).astype(BF16)
    bwd_slots = exchange(pick(bwd_select, normed_b).astype(BF16), experts)

    fwd_select = routing(fwd_ids.reshape(1, tok_count), experts, capacity)
    fwd_values, fwd_scale = normalize(arrived)
    normed_a = (fwd_values * fwd_scale * norm_row).astype(BF16)
    fwd_slots = exchange(pick(fwd_select, normed_a).astype(BF16), experts)

    slot_gate = jnp.sum(
        jnp.where(bwd_select, bwd_gates.reshape(1, tok_count), 0.0), axis=1, keepdims=True
    )
    scaled = (pick(bwd_select, upstream) * slot_gate).astype(BF16)
    grad_slots = exchange(scaled, experts)

    bwd_blocks = ring_gather(bwd_slots)
    fwd_blocks = ring_gather(fwd_slots)
    grad_blocks = ring_gather(grad_slots)

    early, late = [0, 1, -1, 2, -2], [3, -3, 4]
    weights = (gate_mat, up_mat, down_mat)
    fwd_parts = forward_parts(fwd_blocks, early, *weights)
    fwd_parts |= forward_parts(fwd_blocks, late, *weights)
    fwd_back = exchange(ring_reduce(fwd_parts), experts)

    bwd_parts = backward_parts(bwd_blocks, grad_blocks, early, *weights)
    bwd_parts |= backward_parts(bwd_blocks, grad_blocks, late, *weights)
    bwd_back = exchange(ring_reduce(bwd_parts), experts)

    expert_mix = unpick(fwd_select, fwd_back) * fwd_gates.reshape(tok_count, 1)
    forward_result = (fwd_values + expert_mix).astype(BF16)

    grad_norm = unpick(bwd_select, bwd_back)
    scaled_grad = norm_row * grad_norm
    norm_back = bwd_scale * scaled_grad - bwd_values * bwd_scale**3 * jnp.mean(
        bwd_values * scaled_grad, axis=-1, keepdims=True
    )
    backward_result = (upstream.astype(F32) + norm_back).astype(BF16)
    return (forward_result[None], backward_result[None])


def solution(mesh):
    sections, devices = mesh.devices.shape
    slices = devices // max(2, devices // 8)
    grid = Mesh(mesh.devices.reshape(sections, devices // slices, slices), ("pp", "e", "k"))
    tokens = P("pp", ("e", "k"), None)
    weights = P("pp", ("e", "k"), None, None)
    placed = (tokens,) * 7 + (P("pp", None),) + (weights,) * 3
    return jax.shard_map(
        body, mesh=grid, in_specs=placed, out_specs=(tokens, tokens), check_vma=False
    )
```

```python
import functools

import jax
import jax.numpy as jnp
from jax import lax
from jax.experimental import pallas as pl
from jax.experimental.pallas import tpu as pltpu
from jax.sharding import Mesh, PartitionSpec as P

EPSILON = 1e-06
BF16 = jnp.bfloat16
F32 = jnp.float32
CHUNK = 1024
NT = (((1,), (1,)), ((), ()))
TN = (((0,), (0,)), ((), ()))


def shifted(block, axis, distance):
    count = lax.axis_size(axis)
    route = [(i, (i + distance) % count) for i in range(count)]
    return lax.ppermute(block, axis, route)


def call(kernel, outs, *args):
    return pl.pallas_call(
        kernel,
        out_shape=outs,
        in_specs=[pl.BlockSpec(memory_space=pltpu.VMEM)] * len(args),
        out_specs=[pl.BlockSpec(memory_space=pltpu.VMEM)] * len(outs),
        compiler_params=pltpu.CompilerParams(vmem_limit_bytes=12 << 20),
    )(*args)


def like(blocks):
    return [jax.ShapeDtypeStruct(block.shape, block.dtype) for block in blocks]


def chunks(features, step, start):
    def at(i, carry):
        return step(pl.multiple_of(i * CHUNK, CHUNK), carry)

    return lax.fori_loop(0, features // CHUNK, at, start)


def selector(ids_ref, experts, capacity):
    ids = ids_ref[...]
    tok_count = ids.shape[1]
    onehot = (lax.broadcasted_iota(jnp.int32, (experts, tok_count), 0) == ids).astype(F32)
    order = (tok_count, tok_count)
    earlier = lax.broadcasted_iota(jnp.int32, order, 0) < lax.broadcasted_iota(jnp.int32, order, 1)
    before = jnp.dot(onehot, earlier.astype(F32), preferred_element_type=F32)
    slot_index = jnp.sum(before * onehot, axis=0, keepdims=True).astype(jnp.int32)
    target = jnp.where(slot_index < capacity, ids * capacity + slot_index, -1)
    slots = lax.broadcasted_iota(jnp.int32, (experts * capacity, tok_count), 0)
    return (slots == target).astype(F32)


def row_scale(x_ref):
    rows, features = x_ref.shape

    def step(at, total):
        values = x_ref[:, pl.ds(at, CHUNK)].astype(F32)
        return total + jnp.sum(values * values, axis=1, keepdims=True)

    total = chunks(features, step, jnp.zeros((rows, 1), F32))
    return lax.rsqrt(total / features + EPSILON)


def deal(out_ref, at, rows):
    experts, capacity = out_ref.shape[:2]
    for e in range(experts):
        out_ref[e, :, pl.ds(at, CHUNK)] = rows[e * capacity : (e + 1) * capacity].astype(BF16)


def collect(in_ref, at):
    return jnp.concatenate(
        [in_ref[e, :, pl.ds(at, CHUNK)].astype(F32) for e in range(in_ref.shape[0])], axis=0
    )


def norm_slots(x_ref, ids_ref, gain_ref, out_ref, base=0):
    select = selector(ids_ref, *out_ref.shape[:2]).astype(BF16)
    scale = row_scale(x_ref)

    def step(at, carry):
        part = pl.ds(at, CHUNK)
        normed = (x_ref[:, part].astype(F32) * scale * gain_ref[:, part]).astype(BF16)
        deal(out_ref, at + base, jnp.dot(select, normed, preferred_element_type=F32))
        return carry

    chunks(x_ref.shape[1], step, 0)


def scaled_slots(x_ref, ids_ref, gates_ref, out_ref, base):
    select = selector(ids_ref, *out_ref.shape[:2])
    gate = jnp.sum(select * gates_ref[...], axis=1, keepdims=True)
    select = select.astype(BF16)

    def step(at, carry):
        rows = jnp.dot(select, x_ref[:, pl.ds(at, CHUNK)], preferred_element_type=F32)
        deal(out_ref, at + base, rows * gate)
        return carry

    chunks(x_ref.shape[1], step, 0)


def send_kernel(a_ref, a_ids_ref, gain_ref, b_ref, b_ids_ref, b_gates_ref, out_ref):
    norm_slots(a_ref, a_ids_ref, gain_ref, out_ref)
    scaled_slots(b_ref, b_ids_ref, b_gates_ref, out_ref, a_ref.shape[1])


def unpack_kernel(in_ref, *outs):
    features = outs[0].shape[1]
    for n, out in enumerate(outs):

        def step(at, carry, out=out, n=n):
            out[:, pl.ds(at, CHUNK)] = collect(in_ref, at + n * features).astype(BF16)
            return carry

        chunks(features, step, 0)


def total_kernel(*refs):
    out_ref = refs[-1]
    features = refs[0].shape[1]
    for n in range(len(refs) // 3):
        trio = refs[3 * n : 3 * n + 3]

        def step(at, carry, trio=trio, n=n):
            part = pl.ds(at, CHUNK)
            total = sum(ref[:, part].astype(F32) for ref in trio)
            deal(out_ref, at + n * features, total)
            return carry

        chunks(features, step, 0)


def column(row, count):
    diagonal = lax.broadcasted_iota(jnp.int32, (count, count), 0) == lax.broadcasted_iota(
        jnp.int32, (count, count), 1
    )
    return jnp.sum(jnp.where(diagonal, row, 0.0), axis=1, keepdims=True)


def result_kernel(
    back_ref, a_ref, a_ids_ref, a_gates_ref, x_ref, b_ref, b_ids_ref, gain_ref, a_out, b_out, held
):
    rows, features = a_ref.shape
    a_select = selector(a_ids_ref, *back_ref.shape[:2]).astype(BF16)
    b_select = selector(b_ids_ref, *back_ref.shape[:2]).astype(BF16)
    a_gate = column(a_gates_ref[...], rows)

    def first(at, carry):
        squares, products = carry
        part = pl.ds(at, CHUNK)
        mix = lax.dot_general(
            a_select, collect(back_ref, at).astype(BF16), TN, preferred_element_type=F32
        )
        a_out[:, part] = (a_ref[:, part].astype(F32) + mix * a_gate).astype(BF16)
        grad = lax.dot_general(
            b_select, collect(back_ref, at + features).astype(BF16), TN, preferred_element_type=F32
        )
        grad = grad * gain_ref[:, part]
        held[:, part] = grad
        values = x_ref[:, part].astype(F32)
        squares += jnp.sum(values * values, axis=1, keepdims=True)
        products += jnp.sum(values * grad, axis=1, keepdims=True)
        return squares, products

    zero = jnp.zeros((rows, 1), F32)
    squares, products = chunks(features, first, (zero, zero))
    scale = lax.rsqrt(squares / features + EPSILON)
    pull = scale**3 * (products / features)

    def second(at, carry):
        part = pl.ds(at, CHUNK)
        back = scale * held[:, part] - x_ref[:, part].astype(F32) * pull
        b_out[:, part] = (b_ref[:, part].astype(F32) + back).astype(BF16)
        return carry

    chunks(features, second, 0)


def ring_gather(block, far_way):
    far = lax.axis_size("k") // 2
    blocks = {0: block}
    for step in range(1, far):
        for way in (1, -1):
            blocks[-way * step] = shifted(blocks[-way * (step - 1)], "k", way)
    blocks[far] = shifted(blocks[-far_way * (far - 1)], "k", far_way)
    return blocks


def add(a, b):
    return (a.astype(F32) + b.astype(F32)).astype(BF16)


def ring_reduce(parts, far_way):
    far = lax.axis_size("k") // 2
    sums = []
    for way in (far_way, -far_way):
        held = parts[far] if way == far_way else parts[way * (far - 1)]
        for step in range(far - 1 if way == far_way else far - 2, -1, -1):
            held = shifted(held, "k", way)
            if step:
                held = add(held, parts[way * step])
        sums.append(held)
    return [parts[0], *sums]


def stacked(blocks, part):
    return jnp.concatenate([block[:, part].astype(F32) for block in blocks], axis=0).astype(BF16)


def put(outs, part, value):
    at = 0
    for out in outs:
        out[:, part] = value[at : at + out.shape[0]].astype(BF16)
        at += out.shape[0]


def activations(blocks, gate_ref, up_ref):
    features, width = gate_ref.shape
    rows = sum(block.shape[0] for block in blocks)

    def step(at, total):
        part = pl.ds(at, CHUNK)
        right = jnp.concatenate([gate_ref[part, :], up_ref[part, :]], axis=1)
        return total + jnp.dot(stacked(blocks, part), right, preferred_element_type=F32)

    total = chunks(features, step, jnp.zeros((rows, 2 * width), F32))
    return total[:, :width], total[:, width:]


def forward_kernel(count, *refs):
    blocks, outs = refs[:count], refs[count + 3 :]
    gate_ref, up_ref, down_ref = refs[count : count + 3]
    act_gate, act_up = activations(blocks, gate_ref, up_ref)
    hidden = (act_gate * jax.nn.sigmoid(act_gate) * act_up).astype(BF16)

    def step(at, carry):
        part = pl.ds(at, CHUNK)
        put(outs, part, jnp.dot(hidden, down_ref[:, part], preferred_element_type=F32))
        return carry

    chunks(down_ref.shape[1], step, 0)


def act_kernel(count, *refs):
    blocks, (gate_ref, up_ref), outs = refs[:count], refs[count : count + 2], refs[count + 2 :]
    at = 0
    acts = activations(blocks, gate_ref, up_ref)
    for block, gate_out, up_out in zip(blocks, outs[::2], outs[1::2]):
        rows = block.shape[0]
        gate_out[...], up_out[...] = (act[at : at + rows] for act in acts)
        at += rows


def backward_kernel(count, *refs):
    blocks, acts, rest, outs = (
        refs[:count],
        refs[count : 3 * count],
        refs[3 * count : 3 * count + 3],
        refs[3 * count + 3 :],
    )
    gate_ref, up_ref, down_ref = rest
    rows = sum(block.shape[0] for block in blocks)

    def inner(at, total):
        part = pl.ds(at, CHUNK)
        return total + lax.dot_general(
            stacked(blocks, part), down_ref[:, part], NT, preferred_element_type=F32
        )

    zero = jnp.zeros((rows, down_ref.shape[0]), F32)
    back = chunks(down_ref.shape[1], inner, zero)
    act_gate = jnp.concatenate([ref[...] for ref in acts[::2]], axis=0)
    act_up = jnp.concatenate([ref[...] for ref in acts[1::2]], axis=0)
    sigma = jax.nn.sigmoid(act_gate)
    grad_gate = (back * act_up * sigma * (1.0 + act_gate * (1.0 - sigma))).astype(BF16)
    grad_up = (back * act_gate * sigma).astype(BF16)
    left = jnp.concatenate([grad_gate, grad_up], axis=1)

    def outer(at, carry):
        part = pl.ds(at, CHUNK)
        right = jnp.concatenate([gate_ref[part, :], up_ref[part, :]], axis=1)
        put(outs, part, lax.dot_general(left, right, NT, preferred_element_type=F32))
        return carry

    chunks(gate_ref.shape[0], outer, 0)


def forward_parts(blocks, keys, weights):
    rows = [blocks[key] for key in keys]
    outs = call(functools.partial(forward_kernel, len(rows)), like(rows), *rows, *weights)
    return dict(zip(keys, outs))


def gate_and_up(blocks, keys, gate_mat, up_mat):
    rows = [blocks[key] for key in keys]
    width = gate_mat.shape[1]
    outs = [jax.ShapeDtypeStruct((row.shape[0], width), F32) for row in rows for _ in range(2)]
    outs = call(functools.partial(act_kernel, len(rows)), outs, *rows, gate_mat, up_mat)
    return {key: outs[2 * i : 2 * i + 2] for i, key in enumerate(keys)}


def backward_parts(blocks, acts, keys, weights):
    rows = [blocks[key] for key in keys]
    pairs = [act for key in keys for act in acts[key]]
    outs = call(functools.partial(backward_kernel, len(rows)), like(rows), *rows, *pairs, *weights)
    return dict(zip(keys, outs))


def exchange(slots):
    return lax.all_to_all(slots, "e", split_axis=0, concat_axis=0, tiled=True)


def body(
    fwd_in, fwd_ids, fwd_gates, bwd_x, bwd_grad, bwd_ids, bwd_gates, norm_gain, w_gate, w_up, w_down
):
    experts = lax.axis_size("e")
    tok_count, features = fwd_in.shape[1:]
    capacity = max(2, tok_count * fwd_ids.shape[2] // 20)
    weights = gate_mat, up_mat, down_mat = w_gate[0, 0], w_up[0, 0], w_down[0, 0]
    fwd_ids, fwd_gates = fwd_ids.reshape(1, tok_count), fwd_gates.reshape(1, tok_count)
    bwd_ids, bwd_gates = bwd_ids.reshape(1, tok_count), bwd_gates.reshape(1, tok_count)
    bwd_x = bwd_x[0]

    def slots(width):
        return jax.ShapeDtypeStruct((experts, capacity, width), BF16)

    rows = jax.ShapeDtypeStruct((experts * capacity, features), BF16)
    arrived = shifted(fwd_in[0], "pp", 1)
    upstream = shifted(bwd_grad[0], "pp", -1)

    (bwd_send,) = call(norm_slots, [slots(features)], bwd_x, bwd_ids, norm_gain)
    (bwd_slots,) = call(unpack_kernel, [rows], exchange(bwd_send))
    (send,) = call(
        send_kernel,
        [slots(2 * features)],
        *(arrived, fwd_ids, norm_gain, upstream, bwd_ids, bwd_gates),
    )
    fwd_slots, grad_slots = call(unpack_kernel, [rows, rows], exchange(send))

    bwd_blocks = ring_gather(bwd_slots, 1)
    fwd_blocks = ring_gather(fwd_slots, -1)
    grad_blocks = ring_gather(grad_slots, 1)

    near, last = [0, 1, -1, 2, -2, 3, -3], [4]
    fwd_parts = forward_parts(fwd_blocks, near, weights)
    fwd_parts |= forward_parts(fwd_blocks, last, weights)
    fwd_sums = ring_reduce(fwd_parts, -1)

    acts = gate_and_up(bwd_blocks, near + last, gate_mat, up_mat)
    bwd_parts = backward_parts(grad_blocks, acts, near, weights)
    bwd_parts |= backward_parts(grad_blocks, acts, last, weights)
    bwd_sums = ring_reduce(bwd_parts, 1)

    (back,) = call(total_kernel, [slots(2 * features)], *fwd_sums, *bwd_sums)
    back = exchange(back)

    out = jax.ShapeDtypeStruct((tok_count, features), BF16)
    forward_result, backward_result = pl.pallas_call(
        result_kernel,
        out_shape=[out, out],
        in_specs=[pl.BlockSpec(memory_space=pltpu.VMEM)] * 8,
        out_specs=[pl.BlockSpec(memory_space=pltpu.VMEM)] * 2,
        scratch_shapes=[pltpu.VMEM((tok_count, features), F32)],
        compiler_params=pltpu.CompilerParams(vmem_limit_bytes=12 << 20),
    )(back, arrived, fwd_ids, fwd_gates, bwd_x, upstream, bwd_ids, norm_gain)
    return (forward_result[None], backward_result[None])


def solution(mesh):
    sections, devices = mesh.devices.shape
    slices = devices // max(2, devices // 8)
    grid = Mesh(mesh.devices.reshape(sections, devices // slices, slices), ("pp", "e", "k"))
    tokens = P("pp", ("e", "k"), None)
    weights = P("pp", ("e", "k"), None, None)
    placed = (tokens,) * 7 + (P("pp", None),) + (weights,) * 3
    return jax.shard_map(
        body, mesh=grid, in_specs=placed, out_specs=(tokens, tokens), check_vma=False
    )
```

```python
import functools

import jax
import jax.numpy as jnp
from jax import lax
from jax.experimental import pallas as pl
from jax.experimental.pallas import tpu as pltpu
from jax.sharding import Mesh, PartitionSpec as P

EPSILON = 1e-06
BF16 = jnp.bfloat16
F32 = jnp.float32
CHUNK = 1024
NT = (((1,), (1,)), ((), ()))
TN = (((0,), (0,)), ((), ()))


def shifted(block, axis, distance):
    count = lax.axis_size(axis)
    route = [(i, (i + distance) % count) for i in range(count)]
    return lax.ppermute(block, axis, route)


def call(kernel, outs, *args):
    return pl.pallas_call(
        kernel,
        out_shape=outs,
        in_specs=[pl.BlockSpec(memory_space=pltpu.VMEM)] * len(args),
        out_specs=[pl.BlockSpec(memory_space=pltpu.VMEM)] * len(outs),
        compiler_params=pltpu.CompilerParams(vmem_limit_bytes=12 << 20),
    )(*args)


def like(blocks):
    return [jax.ShapeDtypeStruct(block.shape, block.dtype) for block in blocks]


def chunks(features, step, start):
    def at(i, carry):
        return step(pl.multiple_of(i * CHUNK, CHUNK), carry)

    return lax.fori_loop(0, features // CHUNK, at, start)


def selector(ids_ref, experts, capacity):
    ids = ids_ref[...]
    tok_count = ids.shape[1]
    onehot = (lax.broadcasted_iota(jnp.int32, (experts, tok_count), 0) == ids).astype(F32)
    order = (tok_count, tok_count)
    earlier = lax.broadcasted_iota(jnp.int32, order, 0) < lax.broadcasted_iota(jnp.int32, order, 1)
    before = jnp.dot(onehot, earlier.astype(F32), preferred_element_type=F32)
    slot_index = jnp.sum(before * onehot, axis=0, keepdims=True).astype(jnp.int32)
    target = jnp.where(slot_index < capacity, ids * capacity + slot_index, -1)
    slots = lax.broadcasted_iota(jnp.int32, (experts * capacity, tok_count), 0)
    return (slots == target).astype(F32)


def row_scale(x_ref):
    rows, features = x_ref.shape

    def step(at, total):
        values = x_ref[:, pl.ds(at, CHUNK)].astype(F32)
        return total + jnp.sum(values * values, axis=1, keepdims=True)

    total = chunks(features, step, jnp.zeros((rows, 1), F32))
    return lax.rsqrt(total / features + EPSILON)


def deal(out_ref, at, rows):
    experts, capacity = out_ref.shape[:2]
    for e in range(experts):
        out_ref[e, :, pl.ds(at, CHUNK)] = rows[e * capacity : (e + 1) * capacity].astype(BF16)


def collect(in_ref, at):
    return jnp.concatenate(
        [in_ref[e, :, pl.ds(at, CHUNK)].astype(F32) for e in range(in_ref.shape[0])], axis=0
    )


def norm_slots(x_ref, ids_ref, gain_ref, out_ref, base=0):
    select = selector(ids_ref, *out_ref.shape[:2]).astype(BF16)
    scale = row_scale(x_ref)

    def step(at, carry):
        part = pl.ds(at, CHUNK)
        normed = (x_ref[:, part].astype(F32) * scale * gain_ref[:, part]).astype(BF16)
        deal(out_ref, at + base, jnp.dot(select, normed, preferred_element_type=F32))
        return carry

    chunks(x_ref.shape[1], step, 0)


def pick_kernel(experts, a_ref, a_ids_ref, b_ref, b_ids_ref, b_gates_ref, a_out, b_out):
    shape = (experts, a_out.shape[0] // experts)
    a_select = selector(a_ids_ref, *shape).astype(BF16)
    b_select = selector(b_ids_ref, *shape)
    gate = jnp.sum(b_select * b_gates_ref[...], axis=1, keepdims=True)
    b_select = b_select.astype(BF16)

    def step(at, carry):
        part = pl.ds(at, CHUNK)
        a_rows = jnp.dot(a_select, a_ref[:, part], preferred_element_type=F32)
        a_out[:, part] = a_rows.astype(BF16)
        b_rows = jnp.dot(b_select, b_ref[:, part], preferred_element_type=F32)
        b_out[:, part] = (b_rows * gate).astype(BF16)
        return carry

    chunks(a_ref.shape[1], step, 0)


def pack_kernel(a_ref, gain_ref, b_ref, out_ref):
    features = a_ref.shape[1]
    scale = row_scale(a_ref)

    def step(at, carry):
        part = pl.ds(at, CHUNK)
        deal(out_ref, at, a_ref[:, part].astype(F32) * scale * gain_ref[:, part])
        deal(out_ref, at + features, b_ref[:, part])
        return carry

    chunks(features, step, 0)


def unpack_kernel(in_ref, *outs):
    features = outs[0].shape[1]
    for n, out in enumerate(outs):

        def step(at, carry, out=out, n=n):
            out[:, pl.ds(at, CHUNK)] = collect(in_ref, at + n * features).astype(BF16)
            return carry

        chunks(features, step, 0)


def total_kernel(*refs):
    out_ref = refs[-1]
    features = refs[0].shape[1]
    for n in range(len(refs) // 3):
        trio = refs[3 * n : 3 * n + 3]

        def step(at, carry, trio=trio, n=n):
            part = pl.ds(at, CHUNK)
            total = sum(ref[:, part].astype(F32) for ref in trio)
            deal(out_ref, at + n * features, total)
            return carry

        chunks(features, step, 0)


def column(row, count):
    diagonal = lax.broadcasted_iota(jnp.int32, (count, count), 0) == lax.broadcasted_iota(
        jnp.int32, (count, count), 1
    )
    return jnp.sum(jnp.where(diagonal, row, 0.0), axis=1, keepdims=True)


def result_kernel(
    back_ref, a_ref, a_ids_ref, a_gates_ref, x_ref, b_ref, b_ids_ref, gain_ref, a_out, b_out, held
):
    rows, features = a_ref.shape
    a_select = selector(a_ids_ref, *back_ref.shape[:2]).astype(BF16)
    b_select = selector(b_ids_ref, *back_ref.shape[:2]).astype(BF16)
    a_gate = column(a_gates_ref[...], rows)

    def first(at, carry):
        squares, products = carry
        part = pl.ds(at, CHUNK)
        mix = lax.dot_general(
            a_select, collect(back_ref, at).astype(BF16), TN, preferred_element_type=F32
        )
        a_out[:, part] = (a_ref[:, part].astype(F32) + mix * a_gate).astype(BF16)
        grad = lax.dot_general(
            b_select, collect(back_ref, at + features).astype(BF16), TN, preferred_element_type=F32
        )
        grad = grad * gain_ref[:, part]
        held[:, part] = grad
        values = x_ref[:, part].astype(F32)
        squares += jnp.sum(values * values, axis=1, keepdims=True)
        products += jnp.sum(values * grad, axis=1, keepdims=True)
        return squares, products

    zero = jnp.zeros((rows, 1), F32)
    squares, products = chunks(features, first, (zero, zero))
    scale = lax.rsqrt(squares / features + EPSILON)
    pull = scale**3 * (products / features)

    def second(at, carry):
        part = pl.ds(at, CHUNK)
        back = scale * held[:, part] - x_ref[:, part].astype(F32) * pull
        b_out[:, part] = (b_ref[:, part].astype(F32) + back).astype(BF16)
        return carry

    chunks(features, second, 0)


def ring_gather(block, far_way):
    far = lax.axis_size("k") // 2
    blocks = {0: block}
    for step in range(1, far):
        for way in (1, -1):
            blocks[-way * step] = shifted(blocks[-way * (step - 1)], "k", way)
    blocks[far] = shifted(blocks[-far_way * (far - 1)], "k", far_way)
    return blocks


def add(a, b):
    return (a.astype(F32) + b.astype(F32)).astype(BF16)


def ring_reduce(parts, far_way):
    far = lax.axis_size("k") // 2
    sums = []
    for way in (far_way, -far_way):
        held = parts[far] if way == far_way else parts[way * (far - 1)]
        for step in range(far - 1 if way == far_way else far - 2, -1, -1):
            held = shifted(held, "k", way)
            if step:
                held = add(held, parts[way * step])
        sums.append(held)
    return [parts[0], *sums]


def stacked(blocks, part):
    return jnp.concatenate([block[:, part].astype(F32) for block in blocks], axis=0).astype(BF16)


def put(outs, part, value):
    at = 0
    for out in outs:
        out[:, part] = value[at : at + out.shape[0]].astype(BF16)
        at += out.shape[0]


def activations(blocks, gate_ref, up_ref):
    features, width = gate_ref.shape
    rows = sum(block.shape[0] for block in blocks)

    def step(at, total):
        part = pl.ds(at, CHUNK)
        right = jnp.concatenate([gate_ref[part, :], up_ref[part, :]], axis=1)
        return total + jnp.dot(stacked(blocks, part), right, preferred_element_type=F32)

    total = chunks(features, step, jnp.zeros((rows, 2 * width), F32))
    return total[:, :width], total[:, width:]


def forward_kernel(count, *refs):
    blocks, outs = refs[:count], refs[count + 3 :]
    gate_ref, up_ref, down_ref = refs[count : count + 3]
    act_gate, act_up = activations(blocks, gate_ref, up_ref)
    hidden = (act_gate * jax.nn.sigmoid(act_gate) * act_up).astype(BF16)

    def step(at, carry):
        part = pl.ds(at, CHUNK)
        put(outs, part, jnp.dot(hidden, down_ref[:, part], preferred_element_type=F32))
        return carry

    chunks(down_ref.shape[1], step, 0)


def act_kernel(count, *refs):
    blocks, (gate_ref, up_ref), outs = refs[:count], refs[count : count + 2], refs[count + 2 :]
    at = 0
    acts = activations(blocks, gate_ref, up_ref)
    for block, gate_out, up_out in zip(blocks, outs[::2], outs[1::2]):
        rows = block.shape[0]
        gate_out[...], up_out[...] = (act[at : at + rows] for act in acts)
        at += rows


def backward_kernel(count, *refs):
    blocks, acts, rest, outs = (
        refs[:count],
        refs[count : 3 * count],
        refs[3 * count : 3 * count + 3],
        refs[3 * count + 3 :],
    )
    gate_ref, up_ref, down_ref = rest
    rows = sum(block.shape[0] for block in blocks)

    def inner(at, total):
        part = pl.ds(at, CHUNK)
        return total + lax.dot_general(
            stacked(blocks, part), down_ref[:, part], NT, preferred_element_type=F32
        )

    zero = jnp.zeros((rows, down_ref.shape[0]), F32)
    back = chunks(down_ref.shape[1], inner, zero)
    act_gate = jnp.concatenate([ref[...] for ref in acts[::2]], axis=0)
    act_up = jnp.concatenate([ref[...] for ref in acts[1::2]], axis=0)
    sigma = jax.nn.sigmoid(act_gate)
    grad_gate = (back * act_up * sigma * (1.0 + act_gate * (1.0 - sigma))).astype(BF16)
    grad_up = (back * act_gate * sigma).astype(BF16)
    left = jnp.concatenate([grad_gate, grad_up], axis=1)

    def outer(at, carry):
        part = pl.ds(at, CHUNK)
        right = jnp.concatenate([gate_ref[part, :], up_ref[part, :]], axis=1)
        put(outs, part, lax.dot_general(left, right, NT, preferred_element_type=F32))
        return carry

    chunks(gate_ref.shape[0], outer, 0)


def forward_parts(blocks, keys, weights):
    rows = [blocks[key] for key in keys]
    outs = call(functools.partial(forward_kernel, len(rows)), like(rows), *rows, *weights)
    return dict(zip(keys, outs))


def gate_and_up(blocks, keys, gate_mat, up_mat):
    rows = [blocks[key] for key in keys]
    width = gate_mat.shape[1]
    outs = [jax.ShapeDtypeStruct((row.shape[0], width), F32) for row in rows for _ in range(2)]
    outs = call(functools.partial(act_kernel, len(rows)), outs, *rows, gate_mat, up_mat)
    return {key: outs[2 * i : 2 * i + 2] for i, key in enumerate(keys)}


def backward_parts(blocks, acts, keys, weights):
    rows = [blocks[key] for key in keys]
    pairs = [act for key in keys for act in acts[key]]
    outs = call(functools.partial(backward_kernel, len(rows)), like(rows), *rows, *pairs, *weights)
    return dict(zip(keys, outs))


def exchange(slots):
    return lax.all_to_all(slots, "e", split_axis=0, concat_axis=0, tiled=True)


def body(
    fwd_in, fwd_ids, fwd_gates, bwd_x, bwd_grad, bwd_ids, bwd_gates, norm_gain, w_gate, w_up, w_down
):
    experts = lax.axis_size("e")
    tok_count, features = fwd_in.shape[1:]
    capacity = max(2, tok_count * fwd_ids.shape[2] // 20)
    weights = gate_mat, up_mat, down_mat = w_gate[0, 0], w_up[0, 0], w_down[0, 0]
    fwd_ids, fwd_gates = fwd_ids.reshape(1, tok_count), fwd_gates.reshape(1, tok_count)
    bwd_ids, bwd_gates = bwd_ids.reshape(1, tok_count), bwd_gates.reshape(1, tok_count)
    bwd_x = bwd_x[0]

    def slots(width):
        return jax.ShapeDtypeStruct((experts, capacity, width), BF16)

    rows = jax.ShapeDtypeStruct((experts * capacity, features), BF16)
    near_ids = shifted(fwd_ids, "pp", -1)
    far_ids, far_gates = shifted(bwd_ids, "pp", 1), shifted(bwd_gates, "pp", 1)
    (bwd_send,) = call(norm_slots, [slots(features)], bwd_x, bwd_ids, norm_gain)
    (bwd_slots,) = call(unpack_kernel, [rows], exchange(bwd_send))
    fwd_rows, grad_rows = call(
        functools.partial(pick_kernel, experts),
        [rows, rows],
        *(fwd_in[0], near_ids, bwd_grad[0], far_ids, far_gates),
    )
    fwd_rows, grad_rows = shifted(fwd_rows, "pp", 1), shifted(grad_rows, "pp", -1)
    (send,) = call(pack_kernel, [slots(2 * features)], fwd_rows, norm_gain, grad_rows)
    fwd_slots, grad_slots = call(unpack_kernel, [rows, rows], exchange(send))
    arrived = shifted(fwd_in[0], "pp", 1)
    upstream = shifted(bwd_grad[0], "pp", -1)

    bwd_blocks = ring_gather(bwd_slots, 1)
    fwd_blocks = ring_gather(fwd_slots, -1)
    grad_blocks = ring_gather(grad_slots, 1)
    arrived, upstream, fwd_blocks[3] = lax.optimization_barrier(
        (arrived, upstream, fwd_blocks[3])
    )

    keys = list(fwd_blocks)
    fwd_parts = forward_parts(fwd_blocks, keys, weights)
    fwd_sums = ring_reduce(fwd_parts, -1)

    acts = gate_and_up(bwd_blocks, keys, gate_mat, up_mat)
    bwd_parts = backward_parts(grad_blocks, acts, keys, weights)
    bwd_sums = ring_reduce(bwd_parts, 1)

    (back,) = call(total_kernel, [slots(2 * features)], *fwd_sums, *bwd_sums)
    back = exchange(back)

    out = jax.ShapeDtypeStruct((tok_count, features), BF16)
    forward_result, backward_result = pl.pallas_call(
        result_kernel,
        out_shape=[out, out],
        in_specs=[pl.BlockSpec(memory_space=pltpu.VMEM)] * 8,
        out_specs=[pl.BlockSpec(memory_space=pltpu.VMEM)] * 2,
        scratch_shapes=[pltpu.VMEM((tok_count, features), F32)],
        compiler_params=pltpu.CompilerParams(vmem_limit_bytes=12 << 20),
    )(back, arrived, fwd_ids, fwd_gates, bwd_x, upstream, bwd_ids, norm_gain)
    return (forward_result[None], backward_result[None])


def solution(mesh):
    sections, devices = mesh.devices.shape
    slices = devices // max(2, devices // 8)
    grid = Mesh(mesh.devices.reshape(sections, devices // slices, slices), ("pp", "e", "k"))
    tokens = P("pp", ("e", "k"), None)
    weights = P("pp", ("e", "k"), None, None)
    placed = (tokens,) * 7 + (P("pp", None),) + (weights,) * 3
    return jax.shard_map(
        body, mesh=grid, in_specs=placed, out_specs=(tokens, tokens), check_vma=False
    )
```

```python
import functools

import jax
import jax.numpy as jnp
from jax import lax
from jax.experimental import pallas as pl
from jax.experimental.pallas import tpu as pltpu
from jax.sharding import Mesh, PartitionSpec as P

EPSILON = 1e-06
BF16 = jnp.bfloat16
F32 = jnp.float32
CHUNK = 1024
LANES = 128
NT = (((1,), (1,)), ((), ()))


def shifted(block, axis, distance):
    count = lax.axis_size(axis)
    route = [(i, (i + distance) % count) for i in range(count)]
    return lax.ppermute(block, axis, route)


def call(kernel, outs, *args):
    return pl.pallas_call(
        kernel,
        out_shape=outs,
        in_specs=[pl.BlockSpec(memory_space=pltpu.VMEM)] * len(args),
        out_specs=[pl.BlockSpec(memory_space=pltpu.VMEM)] * len(outs),
        compiler_params=pltpu.CompilerParams(vmem_limit_bytes=12 << 20),
    )(*args)


def like(blocks):
    return [jax.ShapeDtypeStruct(block.shape, block.dtype) for block in blocks]


def chunks(features, step, start):
    def at(i, carry):
        return step(pl.multiple_of(i * CHUNK, CHUNK), carry)

    return lax.fori_loop(0, features // CHUNK, at, start)


def selector(ids_ref, experts, capacity):
    ids = ids_ref[...]
    tok_count = ids.shape[1]
    onehot = (lax.broadcasted_iota(jnp.int32, (experts, tok_count), 0) == ids).astype(F32)
    order = (tok_count, tok_count)
    earlier = lax.broadcasted_iota(jnp.int32, order, 0) < lax.broadcasted_iota(jnp.int32, order, 1)
    before = jnp.dot(onehot, earlier.astype(F32), preferred_element_type=F32)
    slot_index = jnp.sum(before * onehot, axis=0, keepdims=True).astype(jnp.int32)
    target = jnp.where(slot_index < capacity, ids * capacity + slot_index, -1)
    slots = lax.broadcasted_iota(jnp.int32, (experts * capacity, tok_count), 0)
    return (slots == target).astype(F32)


def fold(values):
    return sum(values[:, i : i + LANES] for i in range(0, values.shape[1], LANES))


def row_scale(x_ref):
    rows, features = x_ref.shape

    def step(at, total):
        values = x_ref[:, pl.ds(at, CHUNK)].astype(F32)
        return total + fold(values * values)

    total = chunks(features, step, jnp.zeros((rows, LANES), F32))
    return lax.rsqrt(jnp.sum(total, axis=1, keepdims=True) / features + EPSILON)


def deal(out_ref, at, rows):
    experts, capacity = out_ref.shape[:2]
    for e in range(experts):
        out_ref[e, :, pl.ds(at, CHUNK)] = rows[e * capacity : (e + 1) * capacity].astype(BF16)


def collect(in_ref, at):
    return jnp.concatenate(
        [in_ref[e, :, pl.ds(at, CHUNK)].astype(F32) for e in range(in_ref.shape[0])], axis=0
    )


def norm_slots(x_ref, ids_ref, gain_ref, out_ref, base=0):
    select = selector(ids_ref, *out_ref.shape[:2]).astype(BF16)
    scale = row_scale(x_ref)

    def step(at, carry):
        part = pl.ds(at, CHUNK)
        normed = (x_ref[:, part].astype(F32) * scale * gain_ref[:, part]).astype(BF16)
        deal(out_ref, at + base, jnp.dot(select, normed, preferred_element_type=F32))
        return carry

    chunks(x_ref.shape[1], step, 0)


def pick_kernel(experts, a_ref, a_ids_ref, b_ref, b_ids_ref, b_gates_ref, a_out, b_out):
    shape = (experts, a_out.shape[0] // experts)
    a_select = selector(a_ids_ref, *shape).astype(BF16)
    b_select = selector(b_ids_ref, *shape)
    gate = jnp.sum(b_select * b_gates_ref[...], axis=1, keepdims=True)
    b_select = b_select.astype(BF16)

    def step(at, carry):
        part = pl.ds(at, CHUNK)
        a_rows = jnp.dot(a_select, a_ref[:, part], preferred_element_type=F32)
        a_out[:, part] = a_rows.astype(BF16)
        b_rows = jnp.dot(b_select, b_ref[:, part], preferred_element_type=F32)
        b_out[:, part] = (b_rows * gate).astype(BF16)
        return carry

    chunks(a_ref.shape[1], step, 0)


def pack_kernel(a_ref, gain_ref, b_ref, out_ref):
    features = a_ref.shape[1]
    scale = row_scale(a_ref)

    def step(at, carry):
        part = pl.ds(at, CHUNK)
        deal(out_ref, at, a_ref[:, part].astype(F32) * scale * gain_ref[:, part])
        deal(out_ref, at + features, b_ref[:, part])
        return carry

    chunks(features, step, 0)


def unpack_kernel(in_ref, *outs):
    features = outs[0].shape[1]
    for n, out in enumerate(outs):

        def step(at, carry, out=out, n=n):
            out[:, pl.ds(at, CHUNK)] = collect(in_ref, at + n * features).astype(BF16)
            return carry

        chunks(features, step, 0)


def total_kernel(*refs):
    out_ref = refs[-1]
    features = refs[0].shape[1]
    for n in range(len(refs) // 3):
        trio = refs[3 * n : 3 * n + 3]

        def step(at, carry, trio=trio, n=n):
            part = pl.ds(at, CHUNK)
            total = sum(ref[:, part].astype(F32) for ref in trio)
            deal(out_ref, at + n * features, total)
            return carry

        chunks(features, step, 0)


def column(row, count):
    diagonal = lax.broadcasted_iota(jnp.int32, (count, count), 0) == lax.broadcasted_iota(
        jnp.int32, (count, count), 1
    )
    return jnp.sum(jnp.where(diagonal, row, 0.0), axis=1, keepdims=True)


def result_kernel(
    back_ref, a_ref, a_ids_ref, a_gates_ref, x_ref, b_ref, b_ids_ref, gain_ref, a_out, b_out, held
):
    rows, features = a_ref.shape
    a_select = selector(a_ids_ref, *back_ref.shape[:2]).T.astype(BF16)
    b_select = selector(b_ids_ref, *back_ref.shape[:2]).T.astype(BF16)
    a_gate = column(a_gates_ref[...], rows)

    def first(at, carry):
        squares, products = carry
        part = pl.ds(at, CHUNK)
        mix = jnp.dot(a_select, collect(back_ref, at).astype(BF16), preferred_element_type=F32)
        a_out[:, part] = (a_ref[:, part].astype(F32) + mix * a_gate).astype(BF16)
        back = collect(back_ref, at + features).astype(BF16)
        grad = jnp.dot(b_select, back, preferred_element_type=F32) * gain_ref[:, part]
        held[:, part] = grad
        values = x_ref[:, part].astype(F32)
        return squares + fold(values * values), products + fold(values * grad)

    zero = jnp.zeros((rows, LANES), F32)
    squares, products = (
        jnp.sum(total, axis=1, keepdims=True) for total in chunks(features, first, (zero, zero))
    )
    scale = lax.rsqrt(squares / features + EPSILON)
    pull = scale**3 * (products / features)

    def second(at, carry):
        part = pl.ds(at, CHUNK)
        back = scale * held[:, part] - x_ref[:, part].astype(F32) * pull
        b_out[:, part] = (b_ref[:, part].astype(F32) + back).astype(BF16)
        return carry

    chunks(features, second, 0)


def ring_gather(block, far_way):
    far = lax.axis_size("k") // 2
    blocks = {0: block}
    for step in range(1, far):
        for way in (1, -1):
            blocks[-way * step] = shifted(blocks[-way * (step - 1)], "k", way)
    blocks[far] = shifted(blocks[-far_way * (far - 1)], "k", far_way)
    return blocks


def add(a, b):
    return (a.astype(F32) + b.astype(F32)).astype(BF16)


def ring_reduce(parts, far_way):
    far = lax.axis_size("k") // 2
    sums = []
    for way in (far_way, -far_way):
        held = parts[far] if way == far_way else parts[way * (far - 1)]
        for step in range(far - 1 if way == far_way else far - 2, -1, -1):
            held = shifted(held, "k", way)
            if step:
                held = add(held, parts[way * step])
        sums.append(held)
    return [parts[0], *sums]


def stacked(blocks, part):
    return jnp.concatenate([block[:, part].astype(F32) for block in blocks], axis=0).astype(BF16)


def put(outs, part, value):
    at = 0
    for out in outs:
        out[:, part] = value[at : at + out.shape[0]].astype(BF16)
        at += out.shape[0]


def activations(blocks, gate_ref, up_ref):
    features, width = gate_ref.shape
    rows = sum(block.shape[0] for block in blocks)

    def step(at, total):
        part = pl.ds(at, CHUNK)
        right = jnp.concatenate([gate_ref[part, :], up_ref[part, :]], axis=1)
        return total + jnp.dot(stacked(blocks, part), right, preferred_element_type=F32)

    total = chunks(features, step, jnp.zeros((rows, 2 * width), F32))
    return total[:, :width], total[:, width:]


def forward_kernel(count, *refs):
    blocks, outs = refs[:count], refs[count + 3 :]
    gate_ref, up_ref, down_ref = refs[count : count + 3]
    act_gate, act_up = activations(blocks, gate_ref, up_ref)
    hidden = (act_gate * jax.nn.sigmoid(act_gate) * act_up).astype(BF16)

    def step(at, carry):
        part = pl.ds(at, CHUNK)
        put(outs, part, jnp.dot(hidden, down_ref[:, part], preferred_element_type=F32))
        return carry

    chunks(down_ref.shape[1], step, 0)


def act_kernel(count, *refs):
    blocks, (gate_ref, up_ref), outs = refs[:count], refs[count : count + 2], refs[count + 2 :]
    at = 0
    acts = activations(blocks, gate_ref, up_ref)
    for block, gate_out, up_out in zip(blocks, outs[::2], outs[1::2]):
        rows = block.shape[0]
        gate_out[...], up_out[...] = (act[at : at + rows] for act in acts)
        at += rows


def backward_kernel(count, *refs):
    blocks, acts, rest, outs = (
        refs[:count],
        refs[count : 3 * count],
        refs[3 * count : 3 * count + 3],
        refs[3 * count + 3 :],
    )
    gate_ref, up_ref, down_ref = rest
    rows = sum(block.shape[0] for block in blocks)

    def inner(at, total):
        part = pl.ds(at, CHUNK)
        return total + lax.dot_general(
            stacked(blocks, part), down_ref[:, part], NT, preferred_element_type=F32
        )

    zero = jnp.zeros((rows, down_ref.shape[0]), F32)
    back = chunks(down_ref.shape[1], inner, zero)
    act_gate = jnp.concatenate([ref[...] for ref in acts[::2]], axis=0)
    act_up = jnp.concatenate([ref[...] for ref in acts[1::2]], axis=0)
    sigma = jax.nn.sigmoid(act_gate)
    grad_gate = (back * act_up * sigma * (1.0 + act_gate * (1.0 - sigma))).astype(BF16)
    grad_up = (back * act_gate * sigma).astype(BF16)
    left = jnp.concatenate([grad_gate, grad_up], axis=1)

    def outer(at, carry):
        part = pl.ds(at, CHUNK)
        right = jnp.concatenate([gate_ref[part, :], up_ref[part, :]], axis=1)
        put(outs, part, lax.dot_general(left, right, NT, preferred_element_type=F32))
        return carry

    chunks(gate_ref.shape[0], outer, 0)


def forward_parts(blocks, keys, weights):
    rows = [blocks[key] for key in keys]
    outs = call(functools.partial(forward_kernel, len(rows)), like(rows), *rows, *weights)
    return dict(zip(keys, outs))


def gate_and_up(blocks, keys, gate_mat, up_mat):
    rows = [blocks[key] for key in keys]
    width = gate_mat.shape[1]
    outs = [jax.ShapeDtypeStruct((row.shape[0], width), F32) for row in rows for _ in range(2)]
    outs = call(functools.partial(act_kernel, len(rows)), outs, *rows, gate_mat, up_mat)
    return {key: outs[2 * i : 2 * i + 2] for i, key in enumerate(keys)}


def backward_parts(blocks, acts, keys, weights):
    rows = [blocks[key] for key in keys]
    pairs = [act for key in keys for act in acts[key]]
    outs = call(functools.partial(backward_kernel, len(rows)), like(rows), *rows, *pairs, *weights)
    return dict(zip(keys, outs))


def exchange(slots):
    return lax.all_to_all(slots, "e", split_axis=0, concat_axis=0, tiled=True)


def body(
    fwd_in, fwd_ids, fwd_gates, bwd_x, bwd_grad, bwd_ids, bwd_gates, norm_gain, w_gate, w_up, w_down
):
    experts = lax.axis_size("e")
    tok_count, features = fwd_in.shape[1:]
    capacity = max(2, tok_count * fwd_ids.shape[2] // 20)
    weights = gate_mat, up_mat, down_mat = w_gate[0, 0], w_up[0, 0], w_down[0, 0]
    fwd_ids, fwd_gates = fwd_ids.reshape(1, tok_count), fwd_gates.reshape(1, tok_count)
    bwd_ids, bwd_gates = bwd_ids.reshape(1, tok_count), bwd_gates.reshape(1, tok_count)
    bwd_x = bwd_x[0]

    def slots(width):
        return jax.ShapeDtypeStruct((experts, capacity, width), BF16)

    rows = jax.ShapeDtypeStruct((experts * capacity, features), BF16)
    near_ids = shifted(fwd_ids, "pp", -1)
    far_ids, far_gates = shifted(bwd_ids, "pp", 1), shifted(bwd_gates, "pp", 1)
    (bwd_send,) = call(norm_slots, [slots(features)], bwd_x, bwd_ids, norm_gain)
    (bwd_slots,) = call(unpack_kernel, [rows], exchange(bwd_send))
    fwd_rows, grad_rows = call(
        functools.partial(pick_kernel, experts),
        [rows, rows],
        *(fwd_in[0], near_ids, bwd_grad[0], far_ids, far_gates),
    )
    fwd_rows, grad_rows = shifted(fwd_rows, "pp", 1), shifted(grad_rows, "pp", -1)
    (send,) = call(pack_kernel, [slots(2 * features)], fwd_rows, norm_gain, grad_rows)
    fwd_slots, grad_slots = call(unpack_kernel, [rows, rows], exchange(send))
    arrived = shifted(fwd_in[0], "pp", 1)
    upstream = shifted(bwd_grad[0], "pp", -1)

    bwd_blocks = ring_gather(bwd_slots, 1)
    fwd_blocks = ring_gather(fwd_slots, -1)
    grad_blocks = ring_gather(grad_slots, 1)
    arrived, upstream, fwd_blocks[2] = lax.optimization_barrier(
        (arrived, upstream, fwd_blocks[2])
    )

    keys = list(fwd_blocks)
    fwd_parts = forward_parts(fwd_blocks, keys, weights)
    fwd_sums = ring_reduce(fwd_parts, -1)

    acts = gate_and_up(bwd_blocks, keys, gate_mat, up_mat)
    bwd_parts = backward_parts(grad_blocks, acts, keys, weights)
    bwd_sums = ring_reduce(bwd_parts, 1)

    (back,) = call(total_kernel, [slots(2 * features)], *fwd_sums, *bwd_sums)
    back = exchange(back)

    out = jax.ShapeDtypeStruct((tok_count, features), BF16)
    forward_result, backward_result = pl.pallas_call(
        result_kernel,
        out_shape=[out, out],
        in_specs=[pl.BlockSpec(memory_space=pltpu.VMEM)] * 8,
        out_specs=[pl.BlockSpec(memory_space=pltpu.VMEM)] * 2,
        scratch_shapes=[pltpu.VMEM((tok_count, features), F32)],
        compiler_params=pltpu.CompilerParams(vmem_limit_bytes=12 << 20),
    )(back, arrived, fwd_ids, fwd_gates, bwd_x, upstream, bwd_ids, norm_gain)
    return (forward_result[None], backward_result[None])


def solution(mesh):
    sections, devices = mesh.devices.shape
    slices = devices // max(2, devices // 8)
    grid = Mesh(mesh.devices.reshape(sections, devices // slices, slices), ("pp", "e", "k"))
    tokens = P("pp", ("e", "k"), None)
    weights = P("pp", ("e", "k"), None, None)
    placed = (tokens,) * 7 + (P("pp", None),) + (weights,) * 3
    return jax.shard_map(
        body, mesh=grid, in_specs=placed, out_specs=(tokens, tokens), check_vma=False
    )
```

```python
import functools

import jax
import jax.numpy as jnp
from jax import lax
from jax.experimental import pallas as pl
from jax.experimental.pallas import tpu as pltpu
from jax.sharding import Mesh, PartitionSpec as P

EPSILON = 1e-06
BF16 = jnp.bfloat16
F32 = jnp.float32
CHUNK = 1024
LANES = 128
NT = (((1,), (1,)), ((), ()))


def shifted(block, axis, distance):
    count = lax.axis_size(axis)
    route = [(i, (i + distance) % count) for i in range(count)]
    return lax.ppermute(block, axis, route)


def call(kernel, outs, *args):
    return pl.pallas_call(
        kernel,
        out_shape=outs,
        in_specs=[pl.BlockSpec(memory_space=pltpu.VMEM)] * len(args),
        out_specs=[pl.BlockSpec(memory_space=pltpu.VMEM)] * len(outs),
        compiler_params=pltpu.CompilerParams(vmem_limit_bytes=12 << 20),
    )(*args)


def like(blocks):
    return [jax.ShapeDtypeStruct(block.shape, block.dtype) for block in blocks]


def chunks(features, step, start):
    def at(i, carry):
        return step(pl.multiple_of(i * CHUNK, CHUNK), carry)

    return lax.fori_loop(0, features // CHUNK, at, start)


def selector(ids_ref, experts, capacity):
    ids = ids_ref[...]
    tok_count = ids.shape[1]
    onehot = (lax.broadcasted_iota(jnp.int32, (experts, tok_count), 0) == ids).astype(F32)
    order = (tok_count, tok_count)
    earlier = lax.broadcasted_iota(jnp.int32, order, 0) < lax.broadcasted_iota(jnp.int32, order, 1)
    before = jnp.dot(onehot, earlier.astype(F32), preferred_element_type=F32)
    slot_index = jnp.sum(before * onehot, axis=0, keepdims=True).astype(jnp.int32)
    target = jnp.where(slot_index < capacity, ids * capacity + slot_index, -1)
    slots = lax.broadcasted_iota(jnp.int32, (experts * capacity, tok_count), 0)
    return (slots == target).astype(F32)


def fold(values):
    return sum(values[:, i : i + LANES] for i in range(0, values.shape[1], LANES))


def row_scale(x_ref):
    rows, features = x_ref.shape

    def step(at, total):
        values = x_ref[:, pl.ds(at, CHUNK)].astype(F32)
        return total + fold(values * values)

    total = chunks(features, step, jnp.zeros((rows, LANES), F32))
    return lax.rsqrt(jnp.sum(total, axis=1, keepdims=True) / features + EPSILON)


def deal(out_ref, at, rows):
    experts, capacity = out_ref.shape[:2]
    for e in range(experts):
        out_ref[e, :, pl.ds(at, CHUNK)] = rows[e * capacity : (e + 1) * capacity].astype(BF16)


def collect(in_ref, at):
    return jnp.concatenate(
        [in_ref[e, :, pl.ds(at, CHUNK)].astype(F32) for e in range(in_ref.shape[0])], axis=0
    )


def norm_slots(x_ref, ids_ref, gain_ref, out_ref, base=0):
    select = selector(ids_ref, *out_ref.shape[:2]).astype(BF16)
    scale = row_scale(x_ref)

    def step(at, carry):
        part = pl.ds(at, CHUNK)
        normed = (x_ref[:, part].astype(F32) * scale * gain_ref[:, part]).astype(BF16)
        deal(out_ref, at + base, jnp.dot(select, normed, preferred_element_type=F32))
        return carry

    chunks(x_ref.shape[1], step, 0)


def pick_kernel(experts, a_ref, a_ids_ref, b_ref, b_ids_ref, a_out, b_out):
    shape = (experts, a_out.shape[0] // experts)
    a_select = selector(a_ids_ref, *shape).astype(BF16)
    b_select = selector(b_ids_ref, *shape).astype(BF16)

    def step(at, carry):
        part = pl.ds(at, CHUNK)
        a_rows = jnp.dot(a_select, a_ref[:, part], preferred_element_type=F32)
        a_out[:, part] = a_rows.astype(BF16)
        b_rows = jnp.dot(b_select, b_ref[:, part], preferred_element_type=F32)
        b_out[:, part] = b_rows.astype(BF16)
        return carry

    chunks(a_ref.shape[1], step, 0)


def pack_kernel(a_ref, gain_ref, b_ref, ids_ref, gates_ref, out_ref):
    features = a_ref.shape[1]
    select = selector(ids_ref, *out_ref.shape[:2])
    gate = jnp.sum(select * gates_ref[...], axis=1, keepdims=True)
    scale = row_scale(a_ref)

    def step(at, carry):
        part = pl.ds(at, CHUNK)
        deal(out_ref, at, a_ref[:, part].astype(F32) * scale * gain_ref[:, part])
        deal(out_ref, at + features, b_ref[:, part].astype(F32) * gate)
        return carry

    chunks(features, step, 0)


def unpack_kernel(in_ref, *outs):
    features = outs[0].shape[1]
    for n, out in enumerate(outs):

        def step(at, carry, out=out, n=n):
            out[:, pl.ds(at, CHUNK)] = collect(in_ref, at + n * features).astype(BF16)
            return carry

        chunks(features, step, 0)


def total_kernel(*refs):
    out_ref = refs[-1]
    features = refs[0].shape[1]
    for n in range(len(refs) // 3):
        trio = refs[3 * n : 3 * n + 3]

        def step(at, carry, trio=trio, n=n):
            part = pl.ds(at, CHUNK)
            total = sum(ref[:, part].astype(F32) for ref in trio)
            deal(out_ref, at + n * features, total)
            return carry

        chunks(features, step, 0)


def column(row, count):
    diagonal = lax.broadcasted_iota(jnp.int32, (count, count), 0) == lax.broadcasted_iota(
        jnp.int32, (count, count), 1
    )
    return jnp.sum(jnp.where(diagonal, row, 0.0), axis=1, keepdims=True)


def result_kernel(
    back_ref, a_ref, a_ids_ref, a_gates_ref, x_ref, b_ref, b_ids_ref, gain_ref, a_out, b_out, held
):
    rows, features = a_ref.shape
    a_select = selector(a_ids_ref, *back_ref.shape[:2]).T.astype(BF16)
    b_select = selector(b_ids_ref, *back_ref.shape[:2]).T.astype(BF16)
    a_gate = column(a_gates_ref[...], rows)

    def first(at, carry):
        squares, products = carry
        part = pl.ds(at, CHUNK)
        mix = jnp.dot(a_select, collect(back_ref, at).astype(BF16), preferred_element_type=F32)
        a_out[:, part] = (a_ref[:, part].astype(F32) + mix * a_gate).astype(BF16)
        back = collect(back_ref, at + features).astype(BF16)
        grad = jnp.dot(b_select, back, preferred_element_type=F32) * gain_ref[:, part]
        held[:, part] = grad
        values = x_ref[:, part].astype(F32)
        return squares + fold(values * values), products + fold(values * grad)

    zero = jnp.zeros((rows, LANES), F32)
    squares, products = (
        jnp.sum(total, axis=1, keepdims=True) for total in chunks(features, first, (zero, zero))
    )
    scale = lax.rsqrt(squares / features + EPSILON)
    pull = scale**3 * (products / features)

    def second(at, carry):
        part = pl.ds(at, CHUNK)
        back = scale * held[:, part] - x_ref[:, part].astype(F32) * pull
        b_out[:, part] = (b_ref[:, part].astype(F32) + back).astype(BF16)
        return carry

    chunks(features, second, 0)


def ring_gather(block, far_way):
    far = lax.axis_size("k") // 2
    blocks = {0: block}
    for step in range(1, far):
        for way in (1, -1):
            blocks[-way * step] = shifted(blocks[-way * (step - 1)], "k", way)
    blocks[far] = shifted(blocks[-far_way * (far - 1)], "k", far_way)
    return blocks


def add(a, b):
    return (a.astype(F32) + b.astype(F32)).astype(BF16)


def ring_reduce(parts, far_way):
    far = lax.axis_size("k") // 2
    sums = []
    for way in (far_way, -far_way):
        held = parts[far] if way == far_way else parts[way * (far - 1)]
        for step in range(far - 1 if way == far_way else far - 2, -1, -1):
            held = shifted(held, "k", way)
            if step:
                held = add(held, parts[way * step])
        sums.append(held)
    return [parts[0], *sums]


def stacked(blocks, part):
    return jnp.concatenate([block[:, part].astype(F32) for block in blocks], axis=0).astype(BF16)


def put(outs, part, value):
    at = 0
    for out in outs:
        out[:, part] = value[at : at + out.shape[0]].astype(BF16)
        at += out.shape[0]


def activations(blocks, gate_ref, up_ref):
    features, width = gate_ref.shape
    rows = sum(block.shape[0] for block in blocks)

    def step(at, total):
        part = pl.ds(at, CHUNK)
        right = jnp.concatenate([gate_ref[part, :], up_ref[part, :]], axis=1)
        return total + jnp.dot(stacked(blocks, part), right, preferred_element_type=F32)

    total = chunks(features, step, jnp.zeros((rows, 2 * width), F32))
    return total[:, :width], total[:, width:]


def forward_kernel(count, *refs):
    blocks, outs = refs[:count], refs[count + 3 :]
    gate_ref, up_ref, down_ref = refs[count : count + 3]
    act_gate, act_up = activations(blocks, gate_ref, up_ref)
    hidden = (act_gate * jax.nn.sigmoid(act_gate) * act_up).astype(BF16)

    def step(at, carry):
        part = pl.ds(at, CHUNK)
        put(outs, part, jnp.dot(hidden, down_ref[:, part], preferred_element_type=F32))
        return carry

    chunks(down_ref.shape[1], step, 0)


def act_kernel(count, *refs):
    blocks, (gate_ref, up_ref), outs = refs[:count], refs[count : count + 2], refs[count + 2 :]
    at = 0
    acts = activations(blocks, gate_ref, up_ref)
    for block, gate_out, up_out in zip(blocks, outs[::2], outs[1::2]):
        rows = block.shape[0]
        gate_out[...], up_out[...] = (act[at : at + rows] for act in acts)
        at += rows


def backward_kernel(count, *refs):
    blocks, acts, rest, outs = (
        refs[:count],
        refs[count : 3 * count],
        refs[3 * count : 3 * count + 3],
        refs[3 * count + 3 :],
    )
    gate_ref, up_ref, down_ref = rest
    rows = sum(block.shape[0] for block in blocks)

    def inner(at, total):
        part = pl.ds(at, CHUNK)
        return total + lax.dot_general(
            stacked(blocks, part), down_ref[:, part], NT, preferred_element_type=F32
        )

    zero = jnp.zeros((rows, down_ref.shape[0]), F32)
    back = chunks(down_ref.shape[1], inner, zero)
    act_gate = jnp.concatenate([ref[...] for ref in acts[::2]], axis=0)
    act_up = jnp.concatenate([ref[...] for ref in acts[1::2]], axis=0)
    sigma = jax.nn.sigmoid(act_gate)
    grad_gate = (back * act_up * sigma * (1.0 + act_gate * (1.0 - sigma))).astype(BF16)
    grad_up = (back * act_gate * sigma).astype(BF16)
    left = jnp.concatenate([grad_gate, grad_up], axis=1)

    def outer(at, carry):
        part = pl.ds(at, CHUNK)
        right = jnp.concatenate([gate_ref[part, :], up_ref[part, :]], axis=1)
        put(outs, part, lax.dot_general(left, right, NT, preferred_element_type=F32))
        return carry

    chunks(gate_ref.shape[0], outer, 0)


def forward_parts(blocks, keys, weights):
    rows = [blocks[key] for key in keys]
    outs = call(functools.partial(forward_kernel, len(rows)), like(rows), *rows, *weights)
    return dict(zip(keys, outs))


def gate_and_up(blocks, keys, gate_mat, up_mat):
    rows = [blocks[key] for key in keys]
    width = gate_mat.shape[1]
    outs = [jax.ShapeDtypeStruct((row.shape[0], width), F32) for row in rows for _ in range(2)]
    outs = call(functools.partial(act_kernel, len(rows)), outs, *rows, gate_mat, up_mat)
    return {key: outs[2 * i : 2 * i + 2] for i, key in enumerate(keys)}


def backward_parts(blocks, acts, keys, weights):
    rows = [blocks[key] for key in keys]
    pairs = [act for key in keys for act in acts[key]]
    outs = call(functools.partial(backward_kernel, len(rows)), like(rows), *rows, *pairs, *weights)
    return dict(zip(keys, outs))


def exchange(slots):
    return lax.all_to_all(slots, "e", split_axis=0, concat_axis=0, tiled=True)


def body(
    fwd_in, fwd_ids, fwd_gates, bwd_x, bwd_grad, bwd_ids, bwd_gates, norm_gain, w_gate, w_up, w_down
):
    experts = lax.axis_size("e")
    tok_count, features = fwd_in.shape[1:]
    capacity = max(2, tok_count * fwd_ids.shape[2] // 20)
    weights = gate_mat, up_mat, down_mat = w_gate[0, 0], w_up[0, 0], w_down[0, 0]
    fwd_ids, fwd_gates = fwd_ids.reshape(1, tok_count), fwd_gates.reshape(1, tok_count)
    bwd_ids, bwd_gates = bwd_ids.reshape(1, tok_count), bwd_gates.reshape(1, tok_count)
    bwd_x = bwd_x[0]

    def slots(width):
        return jax.ShapeDtypeStruct((experts, capacity, width), BF16)

    rows = jax.ShapeDtypeStruct((experts * capacity, features), BF16)
    near_ids = shifted(fwd_ids, "pp", -1)
    far_ids = shifted(bwd_ids, "pp", 1)
    (bwd_send,) = call(norm_slots, [slots(features)], bwd_x, bwd_ids, norm_gain)
    (bwd_slots,) = call(unpack_kernel, [rows], exchange(bwd_send))
    fwd_rows, grad_rows = call(
        functools.partial(pick_kernel, experts),
        [rows, rows],
        *(fwd_in[0], near_ids, bwd_grad[0], far_ids),
    )
    fwd_rows, grad_rows = shifted(fwd_rows, "pp", 1), shifted(grad_rows, "pp", -1)
    (send,) = call(
        pack_kernel,
        [slots(2 * features)],
        *(fwd_rows, norm_gain, grad_rows, bwd_ids, bwd_gates),
    )
    fwd_slots, grad_slots = call(unpack_kernel, [rows, rows], exchange(send))
    arrived = shifted(fwd_in[0], "pp", 1)
    upstream = shifted(bwd_grad[0], "pp", -1)

    bwd_blocks = ring_gather(bwd_slots, 1)
    fwd_blocks = ring_gather(fwd_slots, -1)
    grad_blocks = ring_gather(grad_slots, 1)
    arrived, upstream, fwd_blocks[2] = lax.optimization_barrier(
        (arrived, upstream, fwd_blocks[2])
    )

    keys = list(fwd_blocks)
    fwd_parts = forward_parts(fwd_blocks, keys, weights)
    fwd_sums = ring_reduce(fwd_parts, -1)

    acts = gate_and_up(bwd_blocks, keys, gate_mat, up_mat)
    bwd_parts = backward_parts(grad_blocks, acts, keys, weights)
    bwd_sums = ring_reduce(bwd_parts, 1)

    (back,) = call(total_kernel, [slots(2 * features)], *fwd_sums, *bwd_sums)
    back = exchange(back)

    out = jax.ShapeDtypeStruct((tok_count, features), BF16)
    forward_result, backward_result = pl.pallas_call(
        result_kernel,
        out_shape=[out, out],
        in_specs=[pl.BlockSpec(memory_space=pltpu.VMEM)] * 8,
        out_specs=[pl.BlockSpec(memory_space=pltpu.VMEM)] * 2,
        scratch_shapes=[pltpu.VMEM((tok_count, features), F32)],
        compiler_params=pltpu.CompilerParams(vmem_limit_bytes=12 << 20),
    )(back, arrived, fwd_ids, fwd_gates, bwd_x, upstream, bwd_ids, norm_gain)
    return (forward_result[None], backward_result[None])


def solution(mesh):
    sections, devices = mesh.devices.shape
    slices = devices // max(2, devices // 8)
    grid = Mesh(mesh.devices.reshape(sections, devices // slices, slices), ("pp", "e", "k"))
    tokens = P("pp", ("e", "k"), None)
    weights = P("pp", ("e", "k"), None, None)
    placed = (tokens,) * 7 + (P("pp", None),) + (weights,) * 3
    return jax.shard_map(
        body, mesh=grid, in_specs=placed, out_specs=(tokens, tokens), check_vma=False
    )
```
